128 devices in a mesh: dom: 16 (over x, y), sub: 8 (over z, core).
Axes of the slice: x: 4, y: 4, z: 4, core: 2. Of those that a mesh axis runs over, the one named last changes fastest.
Arguments:
- node_state: float32 [131072, 128], P(('dom', 'sub')), may hold values from -6 to 6
- edge_state: float32 [524288, 128], P(('dom', 'sub')), may hold values from -6 to 6
- sender: int32 [524288], P(('dom', 'sub')), may hold values from 0 to 1535, as said below
- receiver: int32 [524288], P(('dom', 'sub')), may hold values from 0 to 1023, as said below
- send_rows: int32 [128, 4, 128], P(('dom', 'sub')), may hold values from 0 to 1023
- step_owner: int32 [4], replicated, may hold values from 0 to 127
- edge_weights: float32 [128, 512, 128], P(('dom', 'sub')), may hold values from -0.3125 to 0.3125
- node_weights: float32 [128, 384, 128], P(('dom', 'sub')), may hold values from -0.375 to 0.375
- step_bias: float32 [128, 6, 128], P(('dom', 'sub')), may hold values from -3 to 3
- step_gain: float32 [128, 2, 128], P(('dom', 'sub')), may hold values from 0.25 to 1.75
Outputs:
- node_out: float32 [131072, 128], P(('dom', 'sub'))
- edge_out: float32 [524288, 128], P(('dom', 'sub'))
The draws below stay inside these ranges and needn't reach their ends.
Inputs may be any that keep to these rules, and one draw needn't show every extreme that they name: sender below 1024 names an own node of the edge's device; otherwise it names ghost row k arriving from direction j as 1024 + j * 128 + k. `receiver`: non-decreasing within each device's 4096 edges; the edges w * 512 to w * 512 + 511 of a device have receivers from w * 128 to w * 128 + 127.
All inputs are finite; a program needn't handle non-finite values.
Results may differ from the reference program's by a relative error of at most 0.00015.
Values sent between devices are 32-bit elements; how exact they have to be, the bound alone decides.
A program may use at most 64 MiB of HBM per device.

```python
import jax
import jax.numpy as jnp
from jax import lax

D = 128
WIN = 128
NV_DEV = 1024
NE_DEV = 4096
SLOT = 128
NBR = 4
STEPS = 4
DEVS = 128
NV = 131072
NE = 524288
GHOSTS = 512
N_DOM = 16
N_SUB = 8


def draw_sender(key, part):
    devices = NE // NE_DEV
    keys = jax.random.split(key, 4)
    choose = jax.random.randint(keys[0], (devices, NE_DEV), 0, 4)
    local = jax.random.randint(keys[1], (devices, NE_DEV), 0, NV_DEV)
    remote = NV_DEV + jax.random.randint(keys[2], (devices, NE_DEV), 0, GHOSTS)
    chosen = jnp.where(choose == 0, remote, local)
    column = jax.random.randint(keys[3], (devices, 1), 0, NE_DEV)
    places = jnp.arange(NE_DEV, dtype=jnp.int32)[None, :]
    chosen = jnp.where(places == column, NV_DEV + GHOSTS - 1, chosen)
    return chosen.reshape(-1).astype(jnp.int32)


def draw_receiver(key, part):
    devices = NE // NE_DEV
    windows = NV_DEV // WIN
    per_window = NE_DEV // windows
    keys = jax.random.split(key, 2)
    drawn = jax.random.randint(keys[0], (devices, windows, per_window), 0, WIN)
    column = jax.random.randint(keys[1], (devices, 1, 1), 0, per_window)
    places = jnp.arange(per_window, dtype=jnp.int32)[None, None, :]
    last = (jnp.arange(windows, dtype=jnp.int32) == windows - 1)[None, :, None]
    drawn = jnp.where(jnp.logical_and(places == column, last), WIN - 1, drawn)
    drawn = jnp.sort(drawn, axis=2)
    offsets = (jnp.arange(windows, dtype=jnp.int32) * WIN)[None, :, None]
    return (drawn + offsets).reshape(-1).astype(jnp.int32)


def plant(array, rng, least, high):
    index_at = [jax.random.randint(jax.random.fold_in(rng, axis), (), 0, length) for axis, length in enumerate(array.shape)]
    longest = array.shape.index(max(array.shape))
    neighbour = index_at[:longest] + [(index_at[longest] + 1) % array.shape[longest]] + index_at[longest + 1:]
    return array.at[tuple(index_at)].set(least).at[tuple(neighbour)].set(high)


def levels(stream_key, dims, cuts, smallest, top_value):
    def one(axis_at, shards_of):
        steps = jax.random.uniform(jax.random.fold_in(jax.random.fold_in(stream_key, 6), axis_at), (shards_of,), jnp.float32, smallest / len(cuts), top_value / len(cuts))
        return jnp.repeat(jnp.exp(steps), dims[axis_at] // shards_of).reshape((-1,) + (1,) * (len(dims) - axis_at - 1))

    loudness = one(*cuts[0])
    for cut in cuts[1:]:
        loudness = loudness * one(*cut)
    return loudness


def normal_values(rng, extent, scale, most, cuts=(), kind=jnp.bfloat16):
    values = scale * jax.random.normal(rng, extent, jnp.float32)
    if cuts:
        values = values * levels(rng, extent, cuts, -0.22, 0.18)
    return jnp.clip(values, -most, most).astype(kind)


def setup_inputs(seed: int = 0) -> dict:
    seeds = jax.random.split(jax.random.key(seed), 11)
    return {
        "node_state": normal_values(seeds[0], (NV, D), 1.0, 6.0, ((0, 128),), jnp.float32),
        "edge_state": normal_values(seeds[1], (NE, D), 1.0, 6.0, ((0, 128),), jnp.float32),
        "sender": draw_sender(jax.random.fold_in(seeds[10], 71), 0),
        "receiver": draw_receiver(jax.random.fold_in(seeds[10], 71), 0),
        "send_rows": plant(jax.random.randint(seeds[4], (DEVS, NBR, SLOT), 0, NV_DEV), jax.random.fold_in(seeds[4], 1), 0, NV_DEV - 1).astype(jnp.int32),
        "step_owner": plant(jax.random.randint(seeds[5], (STEPS,), 0, DEVS), jax.random.fold_in(seeds[5], 1), 0, DEVS - 1).astype(jnp.int32),
        "edge_weights": normal_values(seeds[6], (DEVS, 4 * D, D), (3 * D) ** -0.5, 0.3125, ((0, 128),), jnp.float32),
        "node_weights": normal_values(seeds[7], (DEVS, 3 * D, D), (2 * D) ** -0.5, 0.375, ((0, 128),), jnp.float32),
        "step_bias": normal_values(seeds[8], (DEVS, 6, D), 0.5, 3.0, ((0, 128),), jnp.float32),
        "step_gain": jnp.clip(1.0 + 0.15 * jax.random.normal(seeds[9], (DEVS, 2, D), jnp.float32), 0.25, 1.75),
    }


def matmul(operand, matrix):
    return jnp.dot(operand, matrix, precision=lax.Precision.HIGHEST, preferred_element_type=jnp.float32)

def normalize(values, scale_row, shift_row):
    center = values - lax.optimization_barrier(jnp.mean(values, axis=-1, keepdims=True))
    spread = lax.optimization_barrier(jnp.mean(center * center, axis=-1, keepdims=True))
    return center * lax.rsqrt(spread + 1e-05) * scale_row + shift_row

def edge_update(edge_rows, source_rows, target_rows, weights, biases, gains):
    features = edge_rows.shape[1]
    hidden = matmul(edge_rows, weights[:features]) + matmul(source_rows, weights[features:2 * features])
    hidden = hidden + matmul(target_rows, weights[2 * features:3 * features]) + biases[0]
    hidden = jnp.maximum(hidden, 0.0)
    result_rows = matmul(hidden, weights[3 * features:]) + biases[1]
    return edge_rows + normalize(result_rows, gains[0], biases[2])

def node_update(node_rows, incoming, weights, biases, gains):
    features = node_rows.shape[1]
    hidden = matmul(node_rows, weights[:features]) + matmul(incoming, weights[features:2 * features]) + biases[3]
    hidden = jnp.maximum(hidden, 0.0)
    result_rows = matmul(hidden, weights[2 * features:]) + biases[4]
    return node_rows + normalize(result_rows, gains[1], biases[5])

def reference(node_state, edge_state, sender, receiver, send_rows, step_owner, edge_weights, node_weights, step_bias, step_gain):
    devices = send_rows.shape[0]
    directions = send_rows.shape[1]
    slots = send_rows.shape[2]
    rows_dev = node_state.shape[0] // devices
    edges_dev = edge_state.shape[0] // devices
    features = node_state.shape[1]
    home_dev = jnp.repeat(jnp.arange(devices, dtype=jnp.int32), edges_dev)
    home_dom = home_dev // N_SUB
    home_sub = home_dev % N_SUB
    ghost_slot = jnp.maximum(sender - rows_dev, 0).astype(jnp.int32)
    direction = ghost_slot // slots
    within = ghost_slot % slots
    dom_step = jnp.where(direction == 0, -1, jnp.where(direction == 1, 1, 0)).astype(jnp.int32)
    sub_step = jnp.where(direction == 2, -1, jnp.where(direction == 3, 1, 0)).astype(jnp.int32)
    peer_dom = (home_dom + dom_step + N_DOM) % N_DOM
    peer_sub = (home_sub + sub_step + N_SUB) % N_SUB
    peer_dev = (peer_dom * N_SUB + peer_sub).astype(jnp.int32)
    flat_rows = send_rows.reshape(-1)
    remote = peer_dev * rows_dev + flat_rows[(peer_dev * directions + direction) * slots + within]
    source_index = jnp.where(sender < rows_dev, home_dev * rows_dev + sender, remote).astype(jnp.int32)
    target_index = (home_dev * rows_dev + receiver).astype(jnp.int32)
    node_rows = node_state
    edge_rows = edge_state
    for number in range(STEPS):
        owner_index = step_owner[number]
        weights_edge = edge_weights[owner_index]
        weights_node = node_weights[owner_index]
        biases = step_bias[owner_index]
        gains = step_gain[owner_index]

        def per_device(packed):
            block_edges, block_source, block_target = packed
            return edge_update(block_edges, node_rows[block_source], node_rows[block_target], weights_edge, biases, gains)
        edge_rows = lax.map(per_device, (edge_rows.reshape(devices, edges_dev, features), source_index.reshape(devices, edges_dev), target_index.reshape(devices, edges_dev))).reshape(-1, features)
        incoming = jax.ops.segment_sum(edge_rows, target_index, num_segments=node_rows.shape[0])
        node_rows = node_update(node_rows, incoming, weights_node, biases, gains)
    return (node_rows, edge_rows)
```

```python
import jax
import jax.numpy as jnp
from jax import lax
from jax.sharding import PartitionSpec as P

WIN = 128
STEPS = 4
AXES = ("dom", "sub")


def from_behind(block, axis, distance):
    devices = range(lax.axis_size(axis))
    route = [((i - distance) % len(devices), i) for i in devices]
    return lax.ppermute(block, axis, route)


def matmul(operand, matrix):
    return jnp.dot(
        operand, matrix, precision=lax.Precision.HIGHEST, preferred_element_type=jnp.float32
    )


def normalize(values, scale_row, shift_row):
    center = values - jnp.mean(values, axis=-1, keepdims=True)
    spread = jnp.mean(center * center, axis=-1, keepdims=True)
    return center * lax.rsqrt(spread + 1e-05) * scale_row + shift_row


def per_device(
    node_state,
    edge_state,
    sender,
    receiver,
    send_rows,
    step_owner,
    edge_weights,
    node_weights,
    step_bias,
    step_gain,
):
    node_rows = node_state
    edge_rows = edge_state
    rows_dev, features = node_rows.shape
    edges_dev = edge_rows.shape[0]
    directions = send_rows.shape[1]
    slots = send_rows.shape[2]
    windows = rows_dev // WIN
    per_window = edges_dev // windows
    me = lax.axis_index("dom") * lax.axis_size("sub") + lax.axis_index("sub")

    bank = jnp.concatenate([edge_weights[0], node_weights[0], step_bias[0], step_gain[0]], axis=0)
    banks = []
    link = None
    for number in range(STEPS):
        masked = jnp.where(me == step_owner[number], bank, jnp.zeros_like(bank))
        if link is not None:
            masked, _ = lax.optimization_barrier((masked, link))
        link = lax.psum(masked, AXES)
        banks.append(link)

    offsets = (jnp.arange(windows, dtype=jnp.int32) * WIN)[:, None]
    relative = receiver.reshape(windows, per_window) - offsets
    incidence = (relative[:, :, None] == jnp.arange(WIN, dtype=jnp.int32)[None, None, :]).astype(
        jnp.float32
    )
    outgoing_rows = send_rows[0].reshape(-1)
    e_rows = 4 * features
    n_rows = 3 * features
    for number in range(STEPS):
        outgoing = jnp.take(node_rows, outgoing_rows, axis=0).reshape(directions, slots, features)
        dom_lower = from_behind(outgoing[0], "dom", 1)
        dom_upper = from_behind(outgoing[1], "dom", -1)
        sub_lower = from_behind(outgoing[2], "sub", 1)
        sub_upper = from_behind(outgoing[3], "sub", -1)
        arrived = jnp.concatenate([dom_lower, dom_upper, sub_lower, sub_upper], axis=0)

        weights = banks[number]
        w1 = weights[0:features]
        w2 = weights[features : 2 * features]
        w3 = weights[2 * features : 3 * features]
        w4 = weights[3 * features : e_rows]
        u1 = weights[e_rows : e_rows + features]
        u2 = weights[e_rows + features : e_rows + 2 * features]
        u3 = weights[e_rows + 2 * features : e_rows + n_rows]
        biases = weights[e_rows + n_rows : e_rows + n_rows + 6]
        gains = weights[e_rows + n_rows + 6 : e_rows + n_rows + 8]

        own_proj = matmul(node_rows, w2)
        ghost_proj = matmul(arrived, w2)
        source_proj = jnp.take(jnp.concatenate([own_proj, ghost_proj], axis=0), sender, axis=0)
        target_proj = jnp.take(matmul(node_rows, w3), receiver, axis=0)
        hidden = matmul(edge_rows, w1) + source_proj
        hidden = hidden + target_proj + biases[0]
        hidden = jnp.maximum(hidden, 0.0)
        result_rows = matmul(hidden, w4) + biases[1]
        edge_rows = edge_rows + normalize(result_rows, gains[0], biases[2])

        incoming = jnp.einsum(
            "bew,bed->bwd",
            incidence,
            edge_rows.reshape(windows, per_window, features),
            precision=lax.Precision.HIGHEST,
            preferred_element_type=jnp.float32,
        ).reshape(rows_dev, features)
        hidden = matmul(node_rows, u1) + matmul(incoming, u2) + biases[3]
        hidden = jnp.maximum(hidden, 0.0)
        result_rows = matmul(hidden, u3) + biases[4]
        node_rows = node_rows + normalize(result_rows, gains[1], biases[5])
    return (node_rows, edge_rows)


def solution(mesh):
    in_specs = (
        P(AXES, None),
        P(AXES, None),
        P(AXES),
        P(AXES),
        P(AXES, None, None),
        P(),
        P(AXES, None, None),
        P(AXES, None, None),
        P(AXES, None, None),
        P(AXES, None, None),
    )
    out_specs = (P(AXES, None), P(AXES, None))
    return jax.shard_map(
        per_device, mesh=mesh, in_specs=in_specs, out_specs=out_specs, check_vma=False
    )
```

```python
import jax
import jax.numpy as jnp
from jax import lax
from jax.sharding import PartitionSpec as P

WIN = 128
STEPS = 4
AXES = ("dom", "sub")


def from_behind(block, axis, distance):
    devices = range(lax.axis_size(axis))
    route = [((i - distance) % len(devices), i) for i in devices]
    return lax.ppermute(block, axis, route)


def shift(block, axis, size, stride, step):
    count = lax.axis_size(axis)
    route = []
    for i in range(count):
        c = (i // stride) % size
        j = i + (((c + step) % size) - c) * stride
        route.append((i, j))
    return lax.ppermute(block, axis, route)


def spread(block, owner):
    n_sub = lax.axis_size("sub")
    my = {"dom": lax.axis_index("dom"), "sub": lax.axis_index("sub")}
    root = {"dom": owner // n_sub, "sub": owner % n_sub}
    half = block.shape[0] // 2
    for axis, size, stride in (("sub", 2, 1), ("sub", 4, 2), ("dom", 4, 1), ("dom", 4, 4)):
        mine = (my[axis] // stride) % size
        theirs = (root[axis] // stride) % size
        k = (mine - theirs + size) % size
        if size == 2:
            got = shift(block, axis, size, stride, 1)
            block = jnp.where(k == 0, block, got)
            continue
        ahead = shift(block, axis, size, stride, 1)
        behind = shift(block, axis, size, stride, -1)
        block = jnp.where(k == 1, ahead, jnp.where(k == size - 1, behind, block))
        top = shift(block[:half], axis, size, stride, 1)
        bottom = shift(block[half:], axis, size, stride, -1)
        block = jnp.where(k == 2, jnp.concatenate([top, bottom], axis=0), block)
    return block


def select_rows(choice, table):
    first = lax.reduce_precision(table, exponent_bits=8, mantissa_bits=7)
    rest = table - first
    second = lax.reduce_precision(rest, exponent_bits=8, mantissa_bits=7)
    third = lax.reduce_precision(rest - second, exponent_bits=8, mantissa_bits=7)
    parts = jnp.concatenate([first, second, third], axis=-1).astype(jnp.bfloat16)
    picked = jnp.matmul(choice, parts, preferred_element_type=jnp.float32)
    width = table.shape[-1]
    return (picked[..., :width] + picked[..., width : 2 * width]) + picked[..., 2 * width :]


def matmul(operand, matrix):
    return jnp.dot(
        operand, matrix, precision=lax.Precision.HIGHEST, preferred_element_type=jnp.float32
    )


def normalize(values, scale_row, shift_row):
    center = values - jnp.mean(values, axis=-1, keepdims=True)
    spread = jnp.mean(center * center, axis=-1, keepdims=True)
    return center * lax.rsqrt(spread + 1e-05) * scale_row + shift_row


def per_device(
    node_state,
    edge_state,
    sender,
    receiver,
    send_rows,
    step_owner,
    edge_weights,
    node_weights,
    step_bias,
    step_gain,
):
    node_rows = node_state
    edge_rows = edge_state
    rows_dev, features = node_rows.shape
    edges_dev = edge_rows.shape[0]
    directions = send_rows.shape[1]
    slots = send_rows.shape[2]
    windows = rows_dev // WIN
    per_window = edges_dev // windows
    me = lax.axis_index("dom") * lax.axis_size("sub") + lax.axis_index("sub")

    bank = jnp.concatenate([edge_weights[0], node_weights[0], step_bias[0], step_gain[0]], axis=0)
    early = 2
    banks = []
    link = None
    for number in range(early):
        masked = jnp.where(me == step_owner[number], bank, jnp.zeros_like(bank))
        if link is not None:
            masked, _ = lax.optimization_barrier((masked, link))
        link = spread(masked, step_owner[number])
        banks.append(link)
    if STEPS > early:
        me_dom = lax.axis_index("dom")
        n_sub = lax.axis_size("sub")
        row = lax.all_gather(bank, "sub")
        late = []
        for number in range(early, STEPS):
            owner = step_owner[number]
            picked = jnp.take(row, owner % n_sub, axis=0)
            late.append(jnp.where(me_dom == owner // n_sub, picked, jnp.zeros_like(picked)))
        late = lax.psum(jnp.stack(late), "dom")
        banks.extend(late[i] for i in range(STEPS - early))

    offsets = (jnp.arange(windows, dtype=jnp.int32) * WIN)[:, None]
    relative = receiver.reshape(windows, per_window) - offsets
    incidence = (relative[:, :, None] == jnp.arange(WIN, dtype=jnp.int32)[None, None, :]).astype(
        jnp.float32
    )
    outgoing_rows = send_rows[0].reshape(-1)
    lookup_rows = rows_dev + directions * slots
    pick_source = (sender[:, None] == jnp.arange(lookup_rows, dtype=jnp.int32)[None, :]).astype(
        jnp.bfloat16
    )
    pick_target = incidence.astype(jnp.bfloat16)
    e_rows = 4 * features
    n_rows = 3 * features
    for number in range(STEPS):
        outgoing = jnp.take(node_rows, outgoing_rows, axis=0).reshape(directions, slots, features)
        dom_lower = from_behind(outgoing[0], "dom", 1)
        dom_upper = from_behind(outgoing[1], "dom", -1)
        sub_lower = from_behind(outgoing[2], "sub", 1)
        sub_upper = from_behind(outgoing[3], "sub", -1)
        arrived = jnp.concatenate([dom_lower, dom_upper, sub_lower, sub_upper], axis=0)

        weights = banks[number]
        w1 = weights[0:features]
        w2 = weights[features : 2 * features]
        w3 = weights[2 * features : 3 * features]
        w4 = weights[3 * features : e_rows]
        u1 = weights[e_rows : e_rows + features]
        u2 = weights[e_rows + features : e_rows + 2 * features]
        u3 = weights[e_rows + 2 * features : e_rows + n_rows]
        biases = weights[e_rows + n_rows : e_rows + n_rows + 6]
        gains = weights[e_rows + n_rows + 6 : e_rows + n_rows + 8]

        own_proj = matmul(node_rows, w2)
        ghost_proj = matmul(arrived, w2)
        source_proj = select_rows(pick_source, jnp.concatenate([own_proj, ghost_proj], axis=0))
        target_proj = select_rows(
            pick_target, matmul(node_rows, w3).reshape(windows, WIN, features)
        ).reshape(edges_dev, features)
        hidden = matmul(edge_rows, w1) + source_proj
        hidden = hidden + target_proj + biases[0]
        hidden = jnp.maximum(hidden, 0.0)
        result_rows = matmul(hidden, w4) + biases[1]
        edge_rows = edge_rows + normalize(result_rows, gains[0], biases[2])

        incoming = jnp.einsum(
            "bew,bed->bwd",
            incidence,
            edge_rows.reshape(windows, per_window, features),
            precision=lax.Precision.HIGHEST,
            preferred_element_type=jnp.float32,
        ).reshape(rows_dev, features)
        hidden = matmul(node_rows, u1) + matmul(incoming, u2) + biases[3]
        hidden = jnp.maximum(hidden, 0.0)
        result_rows = matmul(hidden, u3) + biases[4]
        node_rows = node_rows + normalize(result_rows, gains[1], biases[5])
    return (node_rows, edge_rows)


def solution(mesh):
    in_specs = (
        P(AXES, None),
        P(AXES, None),
        P(AXES),
        P(AXES),
        P(AXES, None, None),
        P(),
        P(AXES, None, None),
        P(AXES, None, None),
        P(AXES, None, None),
        P(AXES, None, None),
    )
    out_specs = (P(AXES, None), P(AXES, None))
    return jax.shard_map(
        per_device, mesh=mesh, in_specs=in_specs, out_specs=out_specs, check_vma=False
    )
```

```python
import jax
import jax.numpy as jnp
from jax import lax
from jax.sharding import PartitionSpec as P

WIN = 128
STEPS = 4
AXES = ("dom", "sub")


def from_behind(block, axis, distance):
    devices = range(lax.axis_size(axis))
    route = [((i - distance) % len(devices), i) for i in devices]
    return lax.ppermute(block, axis, route)


def select_rows(choice, table):
    first = lax.reduce_precision(table, exponent_bits=8, mantissa_bits=7)
    rest = table - first
    second = lax.reduce_precision(rest, exponent_bits=8, mantissa_bits=7)
    third = lax.reduce_precision(rest - second, exponent_bits=8, mantissa_bits=7)
    parts = jnp.concatenate([first, second, third], axis=-1).astype(jnp.bfloat16)
    picked = jnp.matmul(choice, parts, preferred_element_type=jnp.float32)
    width = table.shape[-1]
    return (picked[..., :width] + picked[..., width : 2 * width]) + picked[..., 2 * width :]


def matmul(operand, matrix):
    return jnp.dot(
        operand, matrix, precision=lax.Precision.HIGHEST, preferred_element_type=jnp.float32
    )


def normalize(values, scale_row, shift_row):
    center = values - jnp.mean(values, axis=-1, keepdims=True)
    spread = jnp.mean(center * center, axis=-1, keepdims=True)
    return center * lax.rsqrt(spread + 1e-05) * scale_row + shift_row


def per_device(
    node_state,
    edge_state,
    sender,
    receiver,
    send_rows,
    step_owner,
    edge_weights,
    node_weights,
    step_bias,
    step_gain,
):
    node_rows = node_state
    edge_rows = edge_state
    rows_dev, features = node_rows.shape
    edges_dev = edge_rows.shape[0]
    directions = send_rows.shape[1]
    slots = send_rows.shape[2]
    windows = rows_dev // WIN
    per_window = edges_dev // windows
    me = lax.axis_index("dom") * lax.axis_size("sub") + lax.axis_index("sub")

    bank = jnp.concatenate([edge_weights[0], node_weights[0], step_bias[0], step_gain[0]], axis=0)
    me_dom = lax.axis_index("dom")
    n_sub = lax.axis_size("sub")
    row = lax.all_gather(bank, "sub")
    picked = []
    for number in range(STEPS):
        owner = step_owner[number]
        column = jnp.take(row, owner % n_sub, axis=0)
        picked.append(jnp.where(me_dom == owner // n_sub, column, jnp.zeros_like(column)))
    banks = lax.psum(jnp.stack(picked), "dom")

    offsets = (jnp.arange(windows, dtype=jnp.int32) * WIN)[:, None]
    relative = receiver.reshape(windows, per_window) - offsets
    incidence = (relative[:, :, None] == jnp.arange(WIN, dtype=jnp.int32)[None, None, :]).astype(
        jnp.float32
    )
    outgoing_rows = send_rows[0].reshape(-1)
    lookup_rows = rows_dev + directions * slots
    pick_source = (sender[:, None] == jnp.arange(lookup_rows, dtype=jnp.int32)[None, :]).astype(
        jnp.bfloat16
    )
    pick_target = incidence.astype(jnp.bfloat16)
    e_rows = 4 * features
    n_rows = 3 * features
    for number in range(STEPS):
        outgoing = jnp.take(node_rows, outgoing_rows, axis=0).reshape(directions, slots, features)
        dom_lower = from_behind(outgoing[0], "dom", 1)
        dom_upper = from_behind(outgoing[1], "dom", -1)
        sub_lower = from_behind(outgoing[2], "sub", 1)
        sub_upper = from_behind(outgoing[3], "sub", -1)
        arrived = jnp.concatenate([dom_lower, dom_upper, sub_lower, sub_upper], axis=0)

        weights = banks[number]
        w1 = weights[0:features]
        w2 = weights[features : 2 * features]
        w3 = weights[2 * features : 3 * features]
        w4 = weights[3 * features : e_rows]
        u1 = weights[e_rows : e_rows + features]
        u2 = weights[e_rows + features : e_rows + 2 * features]
        u3 = weights[e_rows + 2 * features : e_rows + n_rows]
        biases = weights[e_rows + n_rows : e_rows + n_rows + 6]
        gains = weights[e_rows + n_rows + 6 : e_rows + n_rows + 8]

        own_proj = matmul(node_rows, w2)
        ghost_proj = matmul(arrived, w2)
        source_proj = select_rows(pick_source, jnp.concatenate([own_proj, ghost_proj], axis=0))
        target_proj = select_rows(
            pick_target, matmul(node_rows, w3).reshape(windows, WIN, features)
        ).reshape(edges_dev, features)
        hidden = matmul(edge_rows, w1) + source_proj
        hidden = hidden + target_proj + biases[0]
        hidden = jnp.maximum(hidden, 0.0)
        result_rows = matmul(hidden, w4) + biases[1]
        edge_rows = edge_rows + normalize(result_rows, gains[0], biases[2])

        incoming = jnp.einsum(
            "bew,bed->bwd",
            incidence,
            edge_rows.reshape(windows, per_window, features),
            precision=lax.Precision.HIGHEST,
            preferred_element_type=jnp.float32,
        ).reshape(rows_dev, features)
        hidden = matmul(node_rows, u1) + matmul(incoming, u2) + biases[3]
        hidden = jnp.maximum(hidden, 0.0)
        result_rows = matmul(hidden, u3) + biases[4]
        node_rows = node_rows + normalize(result_rows, gains[1], biases[5])
    return (node_rows, edge_rows)


def solution(mesh):
    in_specs = (
        P(AXES, None),
        P(AXES, None),
        P(AXES),
        P(AXES),
        P(AXES, None, None),
        P(),
        P(AXES, None, None),
        P(AXES, None, None),
        P(AXES, None, None),
        P(AXES, None, None),
    )
    out_specs = (P(AXES, None), P(AXES, None))
    return jax.shard_map(
        per_device, mesh=mesh, in_specs=in_specs, out_specs=out_specs, check_vma=False
    )
```

```python
import jax
import jax.numpy as jnp
from jax import lax
from jax.sharding import PartitionSpec as P

WIN = 128
STEPS = 4
AXES = ("dom", "sub")


def from_behind(block, axis, distance):
    devices = range(lax.axis_size(axis))
    route = [((i - distance) % len(devices), i) for i in devices]
    return lax.ppermute(block, axis, route)


def shift(block, axis, size, stride, step):
    count = lax.axis_size(axis)
    route = []
    for i in range(count):
        c = (i // stride) % size
        j = i + (((c + step) % size) - c) * stride
        route.append((i, j))
    return lax.ppermute(block, axis, route)


def spread(block, root):
    mine_all = lax.axis_index("dom")
    half = block.shape[0] // 2
    for size, stride in ((4, 1), (4, 4)):
        mine = (mine_all // stride) % size
        theirs = (root // stride) % size
        k = (mine - theirs + size) % size
        ahead = shift(block, "dom", size, stride, 1)
        behind = shift(block, "dom", size, stride, -1)
        block = jnp.where(k == 1, ahead, jnp.where(k == size - 1, behind, block))
        top = shift(block[:half], "dom", size, stride, 1)
        bottom = shift(block[half:], "dom", size, stride, -1)
        block = jnp.where(k == 2, jnp.concatenate([top, bottom], axis=0), block)
    return block


def select_rows(choice, table):
    first = lax.reduce_precision(table, exponent_bits=8, mantissa_bits=7)
    rest = table - first
    second = lax.reduce_precision(rest, exponent_bits=8, mantissa_bits=7)
    third = lax.reduce_precision(rest - second, exponent_bits=8, mantissa_bits=7)
    parts = jnp.concatenate([first, second, third], axis=-1).astype(jnp.bfloat16)
    picked = jnp.matmul(choice, parts, preferred_element_type=jnp.float32)
    width = table.shape[-1]
    return (picked[..., :width] + picked[..., width : 2 * width]) + picked[..., 2 * width :]


def matmul(operand, matrix):
    return jnp.dot(
        operand, matrix, precision=lax.Precision.HIGHEST, preferred_element_type=jnp.float32
    )


def normalize(values, scale_row, shift_row):
    center = values - jnp.mean(values, axis=-1, keepdims=True)
    spread = jnp.mean(center * center, axis=-1, keepdims=True)
    return center * lax.rsqrt(spread + 1e-05) * scale_row + shift_row


def per_device(
    node_state,
    edge_state,
    sender,
    receiver,
    send_rows,
    step_owner,
    edge_weights,
    node_weights,
    step_bias,
    step_gain,
):
    node_rows = node_state
    edge_rows = edge_state
    rows_dev, features = node_rows.shape
    edges_dev = edge_rows.shape[0]
    directions = send_rows.shape[1]
    slots = send_rows.shape[2]
    windows = rows_dev // WIN
    per_window = edges_dev // windows
    me = lax.axis_index("dom") * lax.axis_size("sub") + lax.axis_index("sub")

    bank = jnp.concatenate([edge_weights[0], node_weights[0], step_bias[0], step_gain[0]], axis=0)
    me_dom = lax.axis_index("dom")
    n_sub = lax.axis_size("sub")
    row = lax.all_gather(bank, "sub")
    columns = [jnp.take(row, step_owner[number] % n_sub, axis=0) for number in range(STEPS)]
    banks = [spread(columns[0], step_owner[0] // n_sub)]
    late = [
        jnp.where(me_dom == step_owner[number] // n_sub, columns[number], jnp.zeros_like(columns[number]))
        for number in range(1, STEPS)
    ]
    late = lax.psum(jnp.stack(late), "dom")
    banks.extend(late[i] for i in range(STEPS - 1))

    offsets = (jnp.arange(windows, dtype=jnp.int32) * WIN)[:, None]
    relative = receiver.reshape(windows, per_window) - offsets
    incidence = (relative[:, :, None] == jnp.arange(WIN, dtype=jnp.int32)[None, None, :]).astype(
        jnp.float32
    )
    outgoing_rows = send_rows[0].reshape(-1)
    lookup_rows = rows_dev + directions * slots
    pick_source = (sender[:, None] == jnp.arange(lookup_rows, dtype=jnp.int32)[None, :]).astype(
        jnp.bfloat16
    )
    pick_target = incidence.astype(jnp.bfloat16)
    e_rows = 4 * features
    n_rows = 3 * features
    for number in range(STEPS):
        outgoing = jnp.take(node_rows, outgoing_rows, axis=0).reshape(directions, slots, features)
        dom_lower = from_behind(outgoing[0], "dom", 1)
        dom_upper = from_behind(outgoing[1], "dom", -1)
        sub_lower = from_behind(outgoing[2], "sub", 1)
        sub_upper = from_behind(outgoing[3], "sub", -1)
        arrived = jnp.concatenate([dom_lower, dom_upper, sub_lower, sub_upper], axis=0)

        weights = banks[number]
        w1 = weights[0:features]
        w2 = weights[features : 2 * features]
        w3 = weights[2 * features : 3 * features]
        w4 = weights[3 * features : e_rows]
        u1 = weights[e_rows : e_rows + features]
        u2 = weights[e_rows + features : e_rows + 2 * features]
        u3 = weights[e_rows + 2 * features : e_rows + n_rows]
        biases = weights[e_rows + n_rows : e_rows + n_rows + 6]
        gains = weights[e_rows + n_rows + 6 : e_rows + n_rows + 8]

        own_proj = matmul(node_rows, w2)
        ghost_proj = matmul(arrived, w2)
        source_proj = select_rows(pick_source, jnp.concatenate([own_proj, ghost_proj], axis=0))
        target_proj = select_rows(
            pick_target, matmul(node_rows, w3).reshape(windows, WIN, features)
        ).reshape(edges_dev, features)
        hidden = matmul(edge_rows, w1) + source_proj
        hidden = hidden + target_proj + biases[0]
        hidden = jnp.maximum(hidden, 0.0)
        result_rows = matmul(hidden, w4) + biases[1]
        edge_rows = edge_rows + normalize(result_rows, gains[0], biases[2])

        incoming = jnp.einsum(
            "bew,bed->bwd",
            incidence,
            edge_rows.reshape(windows, per_window, features),
            precision=lax.Precision.HIGHEST,
            preferred_element_type=jnp.float32,
        ).reshape(rows_dev, features)
        hidden = matmul(node_rows, u1) + matmul(incoming, u2) + biases[3]
        hidden = jnp.maximum(hidden, 0.0)
        result_rows = matmul(hidden, u3) + biases[4]
        node_rows = node_rows + normalize(result_rows, gains[1], biases[5])
    return (node_rows, edge_rows)


def solution(mesh):
    in_specs = (
        P(AXES, None),
        P(AXES, None),
        P(AXES),
        P(AXES),
        P(AXES, None, None),
        P(),
        P(AXES, None, None),
        P(AXES, None, None),
        P(AXES, None, None),
        P(AXES, None, None),
    )
    out_specs = (P(AXES, None), P(AXES, None))
    return jax.shard_map(
        per_device, mesh=mesh, in_specs=in_specs, out_specs=out_specs, check_vma=False
    )
```

```python
import jax
import jax.numpy as jnp
from jax import lax
from jax.sharding import PartitionSpec as P

WIN = 128
STEPS = 4
AXES = ("dom", "sub")


def from_behind(block, axis, distance):
    devices = range(lax.axis_size(axis))
    route = [((i - distance) % len(devices), i) for i in devices]
    return lax.ppermute(block, axis, route)


def shift(block, axis, size, stride, step):
    count = lax.axis_size(axis)
    route = []
    for i in range(count):
        c = (i // stride) % size
        j = i + (((c + step) % size) - c) * stride
        route.append((i, j))
    return lax.ppermute(block, axis, route)


def spread(block, root):
    mine_all = lax.axis_index("dom")
    half = block.shape[0] // 2
    for size, stride in ((4, 1), (4, 4)):
        mine = (mine_all // stride) % size
        theirs = (root // stride) % size
        k = (mine - theirs + size) % size
        ahead = shift(block, "dom", size, stride, 1)
        behind = shift(block, "dom", size, stride, -1)
        block = jnp.where(k == 1, ahead, jnp.where(k == size - 1, behind, block))
        top = shift(block[:half], "dom", size, stride, 1)
        bottom = shift(block[half:], "dom", size, stride, -1)
        block = jnp.where(k == 2, jnp.concatenate([top, bottom], axis=0), block)
    return block


def select_rows(choice, table):
    first = lax.reduce_precision(table, exponent_bits=8, mantissa_bits=7)
    rest = table - first
    second = lax.reduce_precision(rest, exponent_bits=8, mantissa_bits=7)
    third = lax.reduce_precision(rest - second, exponent_bits=8, mantissa_bits=7)
    parts = jnp.concatenate([first, second, third], axis=-1).astype(jnp.bfloat16)
    picked = jnp.matmul(choice, parts, preferred_element_type=jnp.float32)
    width = table.shape[-1]
    return (picked[..., :width] + picked[..., width : 2 * width]) + picked[..., 2 * width :]


def matmul(operand, matrix):
    return jnp.dot(
        operand, matrix, precision=lax.Precision.HIGHEST, preferred_element_type=jnp.float32
    )


def normalize(values, scale_row, shift_row):
    center = values - jnp.mean(values, axis=-1, keepdims=True)
    spread = jnp.mean(center * center, axis=-1, keepdims=True)
    return center * lax.rsqrt(spread + 1e-05) * scale_row + shift_row


def per_device(
    node_state,
    edge_state,
    sender,
    receiver,
    send_rows,
    step_owner,
    edge_weights,
    node_weights,
    step_bias,
    step_gain,
):
    node_rows = node_state
    edge_rows = edge_state
    rows_dev, features = node_rows.shape
    edges_dev = edge_rows.shape[0]
    directions = send_rows.shape[1]
    slots = send_rows.shape[2]
    windows = rows_dev // WIN
    per_window = edges_dev // windows
    me = lax.axis_index("dom") * lax.axis_size("sub") + lax.axis_index("sub")

    bank = jnp.concatenate([edge_weights[0], node_weights[0], step_bias[0], step_gain[0]], axis=0)
    me_dom = lax.axis_index("dom")
    n_sub = lax.axis_size("sub")
    row = lax.all_gather(bank, "sub")
    columns = [jnp.take(row, step_owner[number] % n_sub, axis=0) for number in range(STEPS)]
    banks = [spread(columns[0], step_owner[0] // n_sub)]
    late = [
        jnp.where(me_dom == step_owner[number] // n_sub, columns[number], jnp.zeros_like(columns[number]))
        for number in range(1, STEPS)
    ]
    late = lax.psum(jnp.stack(late), "dom")
    banks.extend(late[i] for i in range(STEPS - 1))

    offsets = (jnp.arange(windows, dtype=jnp.int32) * WIN)[:, None]
    relative = receiver.reshape(windows, per_window) - offsets
    incidence = (relative[:, :, None] == jnp.arange(WIN, dtype=jnp.int32)[None, None, :]).astype(
        jnp.float32
    )
    outgoing_rows = send_rows[0].reshape(-1)
    ghosts = directions * slots
    pick_local = (sender[:, None] == jnp.arange(rows_dev, dtype=jnp.int32)[None, :]).astype(
        jnp.bfloat16
    )
    pick_ghost = (
        sender[:, None] == rows_dev + jnp.arange(ghosts, dtype=jnp.int32)[None, :]
    ).astype(jnp.bfloat16)
    pick_target = incidence.astype(jnp.bfloat16)
    e_rows = 4 * features
    n_rows = 3 * features
    for number in range(STEPS):
        outgoing = jnp.take(node_rows, outgoing_rows, axis=0).reshape(directions, slots, features)
        dom_lower = from_behind(outgoing[0], "dom", 1)
        dom_upper = from_behind(outgoing[1], "dom", -1)
        sub_lower = from_behind(outgoing[2], "sub", 1)
        sub_upper = from_behind(outgoing[3], "sub", -1)
        arrived = jnp.concatenate([dom_lower, dom_upper, sub_lower, sub_upper], axis=0)

        weights = banks[number]
        w1 = weights[0:features]
        w2 = weights[features : 2 * features]
        w3 = weights[2 * features : 3 * features]
        w4 = weights[3 * features : e_rows]
        u1 = weights[e_rows : e_rows + features]
        u2 = weights[e_rows + features : e_rows + 2 * features]
        u3 = weights[e_rows + 2 * features : e_rows + n_rows]
        biases = weights[e_rows + n_rows : e_rows + n_rows + 6]
        gains = weights[e_rows + n_rows + 6 : e_rows + n_rows + 8]

        own_proj = matmul(node_rows, w2)
        ghost_proj = matmul(arrived, w2)
        source_proj = select_rows(pick_local, own_proj) + select_rows(pick_ghost, ghost_proj)
        target_proj = select_rows(
            pick_target, matmul(node_rows, w3).reshape(windows, WIN, features)
        ).reshape(edges_dev, features)
        hidden = matmul(edge_rows, w1) + source_proj
        hidden = hidden + target_proj + biases[0]
        hidden = jnp.maximum(hidden, 0.0)
        result_rows = matmul(hidden, w4) + biases[1]
        edge_rows = edge_rows + normalize(result_rows, gains[0], biases[2])

        incoming = jnp.einsum(
            "bew,bed->bwd",
            incidence,
            edge_rows.reshape(windows, per_window, features),
            precision=lax.Precision.HIGHEST,
            preferred_element_type=jnp.float32,
        ).reshape(rows_dev, features)
        hidden = matmul(node_rows, u1) + matmul(incoming, u2) + biases[3]
        hidden = jnp.maximum(hidden, 0.0)
        result_rows = matmul(hidden, u3) + biases[4]
        node_rows = node_rows + normalize(result_rows, gains[1], biases[5])
    return (node_rows, edge_rows)


def solution(mesh):
    in_specs = (
        P(AXES, None),
        P(AXES, None),
        P(AXES),
        P(AXES),
        P(AXES, None, None),
        P(),
        P(AXES, None, None),
        P(AXES, None, None),
        P(AXES, None, None),
        P(AXES, None, None),
    )
    out_specs = (P(AXES, None), P(AXES, None))
    return jax.shard_map(
        per_device, mesh=mesh, in_specs=in_specs, out_specs=out_specs, check_vma=False
    )
```

```python
import jax
import jax.numpy as jnp
from jax import lax
from jax.sharding import PartitionSpec as P

WIN = 128
STEPS = 4
AXES = ("dom", "sub")


def from_behind(block, axis, distance):
    devices = range(lax.axis_size(axis))
    route = [((i - distance) % len(devices), i) for i in devices]
    return lax.ppermute(block, axis, route)


def shift(block, axis, size, stride, step):
    count = lax.axis_size(axis)
    route = []
    for i in range(count):
        c = (i // stride) % size
        j = i + (((c + step) % size) - c) * stride
        route.append((i, j))
    return lax.ppermute(block, axis, route)


def spread(block, root):
    mine_all = lax.axis_index("dom")
    half = block.shape[0] // 2
    for size, stride in ((4, 1), (4, 4)):
        mine = (mine_all // stride) % size
        theirs = (root // stride) % size
        k = (mine - theirs + size) % size
        ahead = shift(block, "dom", size, stride, 1)
        behind = shift(block, "dom", size, stride, -1)
        block = jnp.where(k == 1, ahead, jnp.where(k == size - 1, behind, block))
        top = shift(block[:half], "dom", size, stride, 1)
        bottom = shift(block[half:], "dom", size, stride, -1)
        block = jnp.where(k == 2, jnp.concatenate([top, bottom], axis=0), block)
    return block


def select_rows(choice, table):
    first = lax.reduce_precision(table, exponent_bits=8, mantissa_bits=7)
    second = lax.reduce_precision(table - first, exponent_bits=8, mantissa_bits=7)
    parts = jnp.concatenate([first, second], axis=-1).astype(jnp.bfloat16)
    picked = jnp.matmul(choice, parts, preferred_element_type=jnp.float32)
    width = table.shape[-1]
    return picked[..., :width] + picked[..., width:]

def matmul(operand, matrix):
    return jnp.dot(
        operand, matrix, precision=lax.Precision.HIGHEST, preferred_element_type=jnp.float32
    )


def normalize(values, scale_row, shift_row):
    center = values - jnp.mean(values, axis=-1, keepdims=True)
    spread = jnp.mean(center * center, axis=-1, keepdims=True)
    return center * lax.rsqrt(spread + 1e-05) * scale_row + shift_row


def per_device(
    node_state,
    edge_state,
    sender,
    receiver,
    send_rows,
    step_owner,
    edge_weights,
    node_weights,
    step_bias,
    step_gain,
):
    node_rows = node_state
    edge_rows = edge_state
    rows_dev, features = node_rows.shape
    edges_dev = edge_rows.shape[0]
    directions = send_rows.shape[1]
    slots = send_rows.shape[2]
    windows = rows_dev // WIN
    per_window = edges_dev // windows
    me = lax.axis_index("dom") * lax.axis_size("sub") + lax.axis_index("sub")

    bank = jnp.concatenate([edge_weights[0], node_weights[0], step_bias[0], step_gain[0]], axis=0)
    me_dom = lax.axis_index("dom")
    n_sub = lax.axis_size("sub")
    row = lax.all_gather(bank, "sub")
    columns = [jnp.take(row, step_owner[number] % n_sub, axis=0) for number in range(STEPS)]
    banks = [spread(columns[0], step_owner[0] // n_sub)]
    late = [
        jnp.where(me_dom == step_owner[number] // n_sub, columns[number], jnp.zeros_like(columns[number]))
        for number in range(1, STEPS)
    ]
    late = lax.psum(jnp.stack(late), "dom")
    banks.extend(late[i] for i in range(STEPS - 1))

    offsets = (jnp.arange(windows, dtype=jnp.int32) * WIN)[:, None]
    relative = receiver.reshape(windows, per_window) - offsets
    incidence = (relative[:, :, None] == jnp.arange(WIN, dtype=jnp.int32)[None, None, :]).astype(
        jnp.float32
    )
    outgoing_rows = send_rows[0].reshape(-1)
    ghosts = directions * slots
    pick_local = (sender[:, None] == jnp.arange(rows_dev, dtype=jnp.int32)[None, :]).astype(
        jnp.bfloat16
    )
    pick_ghost = (
        sender[:, None] == rows_dev + jnp.arange(ghosts, dtype=jnp.int32)[None, :]
    ).astype(jnp.bfloat16)
    pick_target = incidence.astype(jnp.bfloat16)
    e_rows = 4 * features
    n_rows = 3 * features
    for number in range(STEPS):
        outgoing = jnp.take(node_rows, outgoing_rows, axis=0).reshape(directions, slots, features)
        dom_lower = from_behind(outgoing[0], "dom", 1)
        dom_upper = from_behind(outgoing[1], "dom", -1)
        sub_lower = from_behind(outgoing[2], "sub", 1)
        sub_upper = from_behind(outgoing[3], "sub", -1)
        arrived = jnp.concatenate([dom_lower, dom_upper, sub_lower, sub_upper], axis=0)

        weights = banks[number]
        w1 = weights[0:features]
        w2 = weights[features : 2 * features]
        w3 = weights[2 * features : 3 * features]
        w4 = weights[3 * features : e_rows]
        u1 = weights[e_rows : e_rows + features]
        u2 = weights[e_rows + features : e_rows + 2 * features]
        u3 = weights[e_rows + 2 * features : e_rows + n_rows]
        biases = weights[e_rows + n_rows : e_rows + n_rows + 6]
        gains = weights[e_rows + n_rows + 6 : e_rows + n_rows + 8]

        own_proj = matmul(node_rows, w2)
        ghost_proj = matmul(arrived, w2)
        source_proj = select_rows(pick_local, own_proj) + select_rows(pick_ghost, ghost_proj)
        target_proj = select_rows(
            pick_target, matmul(node_rows, w3).reshape(windows, WIN, features)
        ).reshape(edges_dev, features)
        hidden = matmul(edge_rows, w1) + source_proj
        hidden = hidden + target_proj + biases[0]
        hidden = jnp.maximum(hidden, 0.0)
        result_rows = matmul(hidden, w4) + biases[1]
        edge_rows = edge_rows + normalize(result_rows, gains[0], biases[2])

        incoming = jnp.einsum(
            "bew,bed->bwd",
            incidence,
            edge_rows.reshape(windows, per_window, features),
            precision=lax.Precision.HIGHEST,
            preferred_element_type=jnp.float32,
        ).reshape(rows_dev, features)
        hidden = matmul(node_rows, u1) + matmul(incoming, u2) + biases[3]
        hidden = jnp.maximum(hidden, 0.0)
        result_rows = matmul(hidden, u3) + biases[4]
        node_rows = node_rows + normalize(result_rows, gains[1], biases[5])
    return (node_rows, edge_rows)


def solution(mesh):
    in_specs = (
        P(AXES, None),
        P(AXES, None),
        P(AXES),
        P(AXES),
        P(AXES, None, None),
        P(),
        P(AXES, None, None),
        P(AXES, None, None),
        P(AXES, None, None),
        P(AXES, None, None),
    )
    out_specs = (P(AXES, None), P(AXES, None))
    return jax.shard_map(
        per_device, mesh=mesh, in_specs=in_specs, out_specs=out_specs, check_vma=False
    )
```

```python
import jax
import jax.numpy as jnp
from jax import lax
from jax.sharding import PartitionSpec as P

WIN = 128
STEPS = 4
AXES = ("dom", "sub")


def from_behind(block, axis, distance):
    devices = range(lax.axis_size(axis))
    route = [((i - distance) % len(devices), i) for i in devices]
    return lax.ppermute(block, axis, route)


def shift(block, axis, size, stride, step):
    count = lax.axis_size(axis)
    route = []
    for i in range(count):
        c = (i // stride) % size
        j = i + (((c + step) % size) - c) * stride
        route.append((i, j))
    return lax.ppermute(block, axis, route)


def spread(block, root):
    mine_all = lax.axis_index("dom")
    half = block.shape[0] // 2
    for size, stride in ((4, 1), (4, 4)):
        mine = (mine_all // stride) % size
        theirs = (root // stride) % size
        k = (mine - theirs + size) % size
        ahead = shift(block, "dom", size, stride, 1)
        behind = shift(block, "dom", size, stride, -1)
        block = jnp.where(k == 1, ahead, jnp.where(k == size - 1, behind, block))
        top = shift(block[:half], "dom", size, stride, 1)
        bottom = shift(block[half:], "dom", size, stride, -1)
        block = jnp.where(k == 2, jnp.concatenate([top, bottom], axis=0), block)
    return block


def select_rows(choice, table):
    first = lax.reduce_precision(table, exponent_bits=8, mantissa_bits=7)
    second = lax.reduce_precision(table - first, exponent_bits=8, mantissa_bits=7)
    parts = jnp.concatenate([first, second], axis=-1).astype(jnp.bfloat16)
    picked = jnp.matmul(choice, parts, preferred_element_type=jnp.float32)
    width = table.shape[-1]
    return picked[..., :width] + picked[..., width:]

def matmul(operand, matrix):
    return jnp.dot(
        operand, matrix, precision=lax.Precision.HIGH, preferred_element_type=jnp.float32
    )


def normalize(values, scale_row, shift_row):
    center = values - jnp.mean(values, axis=-1, keepdims=True)
    spread = jnp.mean(center * center, axis=-1, keepdims=True)
    return center * lax.rsqrt(spread + 1e-05) * scale_row + shift_row


def per_device(
    node_state,
    edge_state,
    sender,
    receiver,
    send_rows,
    step_owner,
    edge_weights,
    node_weights,
    step_bias,
    step_gain,
):
    node_rows = node_state
    edge_rows = edge_state
    rows_dev, features = node_rows.shape
    edges_dev = edge_rows.shape[0]
    directions = send_rows.shape[1]
    slots = send_rows.shape[2]
    windows = rows_dev // WIN
    per_window = edges_dev // windows
    me = lax.axis_index("dom") * lax.axis_size("sub") + lax.axis_index("sub")

    bank = jnp.concatenate([edge_weights[0], node_weights[0], step_bias[0], step_gain[0]], axis=0)
    me_dom = lax.axis_index("dom")
    n_sub = lax.axis_size("sub")
    row = lax.all_gather(bank, "sub")
    columns = [jnp.take(row, step_owner[number] % n_sub, axis=0) for number in range(STEPS)]
    banks = [spread(columns[0], step_owner[0] // n_sub)]
    late = [
        jnp.where(me_dom == step_owner[number] // n_sub, columns[number], jnp.zeros_like(columns[number]))
        for number in range(1, STEPS)
    ]
    late = lax.psum(jnp.stack(late), "dom")
    banks.extend(late[i] for i in range(STEPS - 1))

    offsets = (jnp.arange(windows, dtype=jnp.int32) * WIN)[:, None]
    relative = receiver.reshape(windows, per_window) - offsets
    incidence = (relative[:, :, None] == jnp.arange(WIN, dtype=jnp.int32)[None, None, :]).astype(
        jnp.float32
    )
    outgoing_rows = send_rows[0].reshape(-1)
    ghosts = directions * slots
    pick_local = (sender[:, None] == jnp.arange(rows_dev, dtype=jnp.int32)[None, :]).astype(
        jnp.bfloat16
    )
    pick_ghost = (
        sender[:, None] == rows_dev + jnp.arange(ghosts, dtype=jnp.int32)[None, :]
    ).astype(jnp.bfloat16)
    pick_target = incidence.astype(jnp.bfloat16)
    e_rows = 4 * features
    n_rows = 3 * features
    for number in range(STEPS):
        outgoing = jnp.take(node_rows, outgoing_rows, axis=0).reshape(directions, slots, features)
        dom_lower = from_behind(outgoing[0], "dom", 1)
        dom_upper = from_behind(outgoing[1], "dom", -1)
        sub_lower = from_behind(outgoing[2], "sub", 1)
        sub_upper = from_behind(outgoing[3], "sub", -1)
        arrived = jnp.concatenate([dom_lower, dom_upper, sub_lower, sub_upper], axis=0)

        weights = banks[number]
        w1 = weights[0:features]
        w2 = weights[features : 2 * features]
        w3 = weights[2 * features : 3 * features]
        w4 = weights[3 * features : e_rows]
        u1 = weights[e_rows : e_rows + features]
        u2 = weights[e_rows + features : e_rows + 2 * features]
        u3 = weights[e_rows + 2 * features : e_rows + n_rows]
        biases = weights[e_rows + n_rows : e_rows + n_rows + 6]
        gains = weights[e_rows + n_rows + 6 : e_rows + n_rows + 8]

        own_proj = matmul(node_rows, w2)
        ghost_proj = matmul(arrived, w2)
        source_proj = select_rows(pick_local, own_proj) + select_rows(pick_ghost, ghost_proj)
        target_proj = select_rows(
            pick_target, matmul(node_rows, w3).reshape(windows, WIN, features)
        ).reshape(edges_dev, features)
        hidden = matmul(edge_rows, w1) + source_proj
        hidden = hidden + target_proj + biases[0]
        hidden = jnp.maximum(hidden, 0.0)
        result_rows = matmul(hidden, w4) + biases[1]
        edge_rows = edge_rows + normalize(result_rows, gains[0], biases[2])

        incoming = jnp.einsum(
            "bew,bed->bwd",
            incidence,
            edge_rows.reshape(windows, per_window, features),
            precision=lax.Precision.HIGHEST,
            preferred_element_type=jnp.float32,
        ).reshape(rows_dev, features)
        hidden = matmul(node_rows, u1) + matmul(incoming, u2) + biases[3]
        hidden = jnp.maximum(hidden, 0.0)
        result_rows = matmul(hidden, u3) + biases[4]
        node_rows = node_rows + normalize(result_rows, gains[1], biases[5])
    return (node_rows, edge_rows)


def solution(mesh):
    in_specs = (
        P(AXES, None),
        P(AXES, None),
        P(AXES),
        P(AXES),
        P(AXES, None, None),
        P(),
        P(AXES, None, None),
        P(AXES, None, None),
        P(AXES, None, None),
        P(AXES, None, None),
    )
    out_specs = (P(AXES, None), P(AXES, None))
    return jax.shard_map(
        per_device, mesh=mesh, in_specs=in_specs, out_specs=out_specs, check_vma=False
    )
```

```python
import jax
import jax.numpy as jnp
from jax import lax
from jax.sharding import PartitionSpec as P

WIN = 128
STEPS = 4
AXES = ("dom", "sub")


def from_behind(block, axis, distance):
    devices = range(lax.axis_size(axis))
    route = [((i - distance) % len(devices), i) for i in devices]
    return lax.ppermute(block, axis, route)


def shift(block, axis, size, stride, step):
    count = lax.axis_size(axis)
    route = []
    for i in range(count):
        c = (i // stride) % size
        j = i + (((c + step) % size) - c) * stride
        route.append((i, j))
    return lax.ppermute(block, axis, route)


def spread(block, root):
    mine_all = lax.axis_index("dom")
    half = block.shape[0] // 2
    for size, stride in ((4, 1), (4, 4)):
        mine = (mine_all // stride) % size
        theirs = (root // stride) % size
        k = (mine - theirs + size) % size
        ahead = shift(block, "dom", size, stride, 1)
        behind = shift(block, "dom", size, stride, -1)
        block = jnp.where(k == 1, ahead, jnp.where(k == size - 1, behind, block))
        top = shift(block[:half], "dom", size, stride, 1)
        bottom = shift(block[half:], "dom", size, stride, -1)
        block = jnp.where(k == 2, jnp.concatenate([top, bottom], axis=0), block)
    return block


def select_rows(choice, table):
    first = lax.reduce_precision(table, exponent_bits=8, mantissa_bits=7)
    second = lax.reduce_precision(table - first, exponent_bits=8, mantissa_bits=7)
    parts = jnp.concatenate([first, second], axis=-1).astype(jnp.bfloat16)
    picked = jnp.matmul(choice, parts, preferred_element_type=jnp.float32)
    width = table.shape[-1]
    return picked[..., :width] + picked[..., width:]

def matmul(operand, matrix):
    return jnp.dot(
        operand, matrix, precision=lax.Precision.HIGH, preferred_element_type=jnp.float32
    )


def normalize(values, scale_row, shift_row):
    center = values - jnp.mean(values, axis=-1, keepdims=True)
    spread = jnp.mean(center * center, axis=-1, keepdims=True)
    return center * lax.rsqrt(spread + 1e-05) * scale_row + shift_row


def per_device(
    node_state,
    edge_state,
    sender,
    receiver,
    send_rows,
    step_owner,
    edge_weights,
    node_weights,
    step_bias,
    step_gain,
):
    node_rows = node_state
    edge_rows = edge_state
    rows_dev, features = node_rows.shape
    edges_dev = edge_rows.shape[0]
    directions = send_rows.shape[1]
    slots = send_rows.shape[2]
    windows = rows_dev // WIN
    per_window = edges_dev // windows
    me = lax.axis_index("dom") * lax.axis_size("sub") + lax.axis_index("sub")

    bank = jnp.concatenate([edge_weights[0], node_weights[0], step_bias[0], step_gain[0]], axis=0)
    me_dom = lax.axis_index("dom")
    n_sub = lax.axis_size("sub")
    row = lax.all_gather(bank, "sub")
    columns = [jnp.take(row, step_owner[number] % n_sub, axis=0) for number in range(STEPS)]
    banks = [spread(columns[0], step_owner[0] // n_sub)]
    late = [
        jnp.where(me_dom == step_owner[number] // n_sub, columns[number], jnp.zeros_like(columns[number]))
        for number in range(1, STEPS)
    ]
    late = lax.psum(jnp.stack(late), "dom")
    banks.extend(late[i] for i in range(STEPS - 1))

    offsets = (jnp.arange(windows, dtype=jnp.int32) * WIN)[:, None]
    relative = receiver.reshape(windows, per_window) - offsets
    incidence = (relative[:, :, None] == jnp.arange(WIN, dtype=jnp.int32)[None, None, :]).astype(
        jnp.float32
    )
    outgoing_rows = send_rows[0].reshape(-1)
    ghosts = directions * slots
    pick_local = (sender[:, None] == jnp.arange(rows_dev, dtype=jnp.int32)[None, :]).astype(
        jnp.bfloat16
    )
    pick_ghost = (
        sender[:, None] == rows_dev + jnp.arange(ghosts, dtype=jnp.int32)[None, :]
    ).astype(jnp.bfloat16)
    pick_target = incidence.astype(jnp.bfloat16)
    e_rows = 4 * features
    n_rows = 3 * features
    outgoing = jnp.take(node_rows, outgoing_rows, axis=0)
    for number in range(STEPS):
        outgoing = outgoing.reshape(directions, slots, features)
        dom_lower = from_behind(outgoing[0], "dom", 1)
        dom_upper = from_behind(outgoing[1], "dom", -1)
        sub_lower = from_behind(outgoing[2], "sub", 1)
        sub_upper = from_behind(outgoing[3], "sub", -1)
        arrived = jnp.concatenate([dom_lower, dom_upper, sub_lower, sub_upper], axis=0)

        weights = banks[number]
        w1 = weights[0:features]
        w2 = weights[features : 2 * features]
        w3 = weights[2 * features : 3 * features]
        w4 = weights[3 * features : e_rows]
        u1 = weights[e_rows : e_rows + features]
        u2 = weights[e_rows + features : e_rows + 2 * features]
        u3 = weights[e_rows + 2 * features : e_rows + n_rows]
        biases = weights[e_rows + n_rows : e_rows + n_rows + 6]
        gains = weights[e_rows + n_rows + 6 : e_rows + n_rows + 8]

        own_proj = matmul(node_rows, w2)
        ghost_proj = matmul(arrived, w2)
        source_proj = select_rows(pick_local, own_proj) + select_rows(pick_ghost, ghost_proj)
        target_proj = select_rows(
            pick_target, matmul(node_rows, w3).reshape(windows, WIN, features)
        ).reshape(edges_dev, features)
        hidden = matmul(edge_rows, w1) + source_proj
        hidden = hidden + target_proj + biases[0]
        hidden = jnp.maximum(hidden, 0.0)
        result_rows = matmul(hidden, w4) + biases[1]
        edge_rows = edge_rows + normalize(result_rows, gains[0], biases[2])

        incoming = jnp.einsum(
            "bew,bed->bwd",
            incidence,
            edge_rows.reshape(windows, per_window, features),
            precision=lax.Precision.HIGHEST,
            preferred_element_type=jnp.float32,
        ).reshape(rows_dev, features)

        def node_update(rows, summed):
            hidden = matmul(rows, u1) + matmul(summed, u2) + biases[3]
            hidden = jnp.maximum(hidden, 0.0)
            result_rows = matmul(hidden, u3) + biases[4]
            return rows + normalize(result_rows, gains[1], biases[5])

        if number + 1 < STEPS:
            outgoing = node_update(
                jnp.take(node_rows, outgoing_rows, axis=0), jnp.take(incoming, outgoing_rows, axis=0)
            )
        node_rows = node_update(node_rows, incoming)
    return (node_rows, edge_rows)


def solution(mesh):
    in_specs = (
        P(AXES, None),
        P(AXES, None),
        P(AXES),
        P(AXES),
        P(AXES, None, None),
        P(),
        P(AXES, None, None),
        P(AXES, None, None),
        P(AXES, None, None),
        P(AXES, None, None),
    )
    out_specs = (P(AXES, None), P(AXES, None))
    return jax.shard_map(
        per_device, mesh=mesh, in_specs=in_specs, out_specs=out_specs, check_vma=False
    )
```

```python
import jax
import jax.numpy as jnp
from jax import lax
from jax.sharding import PartitionSpec as P

WIN = 128
STEPS = 4
AXES = ("dom", "sub")


def from_behind(block, axis, distance):
    devices = range(lax.axis_size(axis))
    route = [((i - distance) % len(devices), i) for i in devices]
    return lax.ppermute(block, axis, route)


def shift(block, axis, size, stride, step):
    count = lax.axis_size(axis)
    route = []
    for i in range(count):
        c = (i // stride) % size
        j = i + (((c + step) % size) - c) * stride
        route.append((i, j))
    return lax.ppermute(block, axis, route)


def spread(block, root):
    mine_all = lax.axis_index("dom")
    half = block.shape[0] // 2
    for size, stride in ((4, 1), (4, 4)):
        mine = (mine_all // stride) % size
        theirs = (root // stride) % size
        k = (mine - theirs + size) % size
        ahead = shift(block, "dom", size, stride, 1)
        behind = shift(block, "dom", size, stride, -1)
        block = jnp.where(k == 1, ahead, jnp.where(k == size - 1, behind, block))
        top = shift(block[:half], "dom", size, stride, 1)
        bottom = shift(block[half:], "dom", size, stride, -1)
        block = jnp.where(k == 2, jnp.concatenate([top, bottom], axis=0), block)
    return block


def select_rows(choice, table):
    first = lax.reduce_precision(table, exponent_bits=8, mantissa_bits=7)
    second = lax.reduce_precision(table - first, exponent_bits=8, mantissa_bits=7)
    parts = jnp.concatenate([first, second], axis=-1).astype(jnp.bfloat16)
    picked = jnp.matmul(choice, parts, preferred_element_type=jnp.float32)
    width = table.shape[-1]
    return picked[..., :width] + picked[..., width:]

def matmul(operand, matrix):
    return jnp.dot(
        operand, matrix, precision=lax.Precision.HIGH, preferred_element_type=jnp.float32
    )


def normalize(values, scale_row, shift_row):
    center = values - jnp.mean(values, axis=-1, keepdims=True)
    spread = jnp.mean(center * center, axis=-1, keepdims=True)
    return center * lax.rsqrt(spread + 1e-05) * scale_row + shift_row


def per_device(
    node_state,
    edge_state,
    sender,
    receiver,
    send_rows,
    step_owner,
    edge_weights,
    node_weights,
    step_bias,
    step_gain,
):
    node_rows = node_state
    edge_rows = edge_state
    rows_dev, features = node_rows.shape
    edges_dev = edge_rows.shape[0]
    directions = send_rows.shape[1]
    slots = send_rows.shape[2]
    windows = rows_dev // WIN
    per_window = edges_dev // windows
    me = lax.axis_index("dom") * lax.axis_size("sub") + lax.axis_index("sub")

    bank = jnp.concatenate([edge_weights[0], node_weights[0], step_bias[0], step_gain[0]], axis=0)
    me_dom = lax.axis_index("dom")
    n_sub = lax.axis_size("sub")
    row = lax.all_gather(bank, "sub")
    columns = [jnp.take(row, step_owner[number] % n_sub, axis=0) for number in range(STEPS)]
    banks = [spread(columns[0], step_owner[0] // n_sub)]
    late = [
        jnp.where(me_dom == step_owner[number] // n_sub, columns[number], jnp.zeros_like(columns[number]))
        for number in range(1, STEPS)
    ]
    late = lax.psum(jnp.stack(late), "dom")

    offsets = (jnp.arange(windows, dtype=jnp.int32) * WIN)[:, None]
    relative = receiver.reshape(windows, per_window) - offsets
    incidence = (relative[:, :, None] == jnp.arange(WIN, dtype=jnp.int32)[None, None, :]).astype(
        jnp.float32
    )
    outgoing_rows = send_rows[0].reshape(-1)
    ghosts = directions * slots
    pick_local = (sender[:, None] == jnp.arange(rows_dev, dtype=jnp.int32)[None, :]).astype(
        jnp.bfloat16
    )
    pick_ghost = (
        sender[:, None] == rows_dev + jnp.arange(ghosts, dtype=jnp.int32)[None, :]
    ).astype(jnp.bfloat16)
    pick_target = incidence.astype(jnp.bfloat16)
    e_rows = 4 * features
    n_rows = 3 * features
    def step(node_rows, edge_rows, weights):
        outgoing = jnp.take(node_rows, outgoing_rows, axis=0).reshape(directions, slots, features)
        dom_lower = from_behind(outgoing[0], "dom", 1)
        dom_upper = from_behind(outgoing[1], "dom", -1)
        sub_lower = from_behind(outgoing[2], "sub", 1)
        sub_upper = from_behind(outgoing[3], "sub", -1)
        arrived = jnp.concatenate([dom_lower, dom_upper, sub_lower, sub_upper], axis=0)

        w1 = weights[0:features]
        w2 = weights[features : 2 * features]
        w3 = weights[2 * features : 3 * features]
        w4 = weights[3 * features : e_rows]
        u1 = weights[e_rows : e_rows + features]
        u2 = weights[e_rows + features : e_rows + 2 * features]
        u3 = weights[e_rows + 2 * features : e_rows + n_rows]
        biases = weights[e_rows + n_rows : e_rows + n_rows + 6]
        gains = weights[e_rows + n_rows + 6 : e_rows + n_rows + 8]

        own_proj = matmul(node_rows, w2)
        ghost_proj = matmul(arrived, w2)
        source_proj = select_rows(pick_local, own_proj) + select_rows(pick_ghost, ghost_proj)
        target_proj = select_rows(
            pick_target, matmul(node_rows, w3).reshape(windows, WIN, features)
        ).reshape(edges_dev, features)
        hidden = matmul(edge_rows, w1) + source_proj
        hidden = hidden + target_proj + biases[0]
        hidden = jnp.maximum(hidden, 0.0)
        result_rows = matmul(hidden, w4) + biases[1]
        edge_rows = edge_rows + normalize(result_rows, gains[0], biases[2])

        incoming = jnp.einsum(
            "bew,bed->bwd",
            incidence,
            edge_rows.reshape(windows, per_window, features),
            precision=lax.Precision.HIGHEST,
            preferred_element_type=jnp.float32,
        ).reshape(rows_dev, features)
        hidden = matmul(node_rows, u1) + matmul(incoming, u2) + biases[3]
        hidden = jnp.maximum(hidden, 0.0)
        result_rows = matmul(hidden, u3) + biases[4]
        node_rows = node_rows + normalize(result_rows, gains[1], biases[5])
        return node_rows, edge_rows

    node_rows, edge_rows = step(node_rows, edge_rows, banks[0])

    def loop_body(carry, weights):
        return step(*carry, weights), None

    (node_rows, edge_rows), _ = lax.scan(loop_body, (node_rows, edge_rows), late)
    return (node_rows, edge_rows)


def solution(mesh):
    in_specs = (
        P(AXES, None),
        P(AXES, None),
        P(AXES),
        P(AXES),
        P(AXES, None, None),
        P(),
        P(AXES, None, None),
        P(AXES, None, None),
        P(AXES, None, None),
        P(AXES, None, None),
    )
    out_specs = (P(AXES, None), P(AXES, None))
    return jax.shard_map(
        per_device, mesh=mesh, in_specs=in_specs, out_specs=out_specs, check_vma=False
    )
```

```python
import jax
import jax.numpy as jnp
from jax import lax
from jax.sharding import PartitionSpec as P

WIN = 128
STEPS = 4
AXES = ("dom", "sub")


def from_behind(block, axis, distance):
    devices = range(lax.axis_size(axis))
    route = [((i - distance) % len(devices), i) for i in devices]
    return lax.ppermute(block, axis, route)


def shift(block, axis, size, stride, step):
    count = lax.axis_size(axis)
    route = []
    for i in range(count):
        c = (i // stride) % size
        j = i + (((c + step) % size) - c) * stride
        route.append((i, j))
    return lax.ppermute(block, axis, route)


def spread(block, root):
    mine_all = lax.axis_index("dom")
    half = block.shape[0] // 2
    for size, stride in ((4, 1), (4, 4)):
        mine = (mine_all // stride) % size
        theirs = (root // stride) % size
        k = (mine - theirs + size) % size
        ahead = shift(block, "dom", size, stride, 1)
        behind = shift(block, "dom", size, stride, -1)
        block = jnp.where(k == 1, ahead, jnp.where(k == size - 1, behind, block))
        top = shift(block[:half], "dom", size, stride, 1)
        bottom = shift(block[half:], "dom", size, stride, -1)
        block = jnp.where(k == 2, jnp.concatenate([top, bottom], axis=0), block)
    return block


def select_rows(choice, table):
    first = lax.reduce_precision(table, exponent_bits=8, mantissa_bits=7)
    second = lax.reduce_precision(table - first, exponent_bits=8, mantissa_bits=7)
    parts = jnp.concatenate([first, second], axis=-1).astype(jnp.bfloat16)
    picked = jnp.matmul(choice, parts, preferred_element_type=jnp.float32)
    width = table.shape[-1]
    return picked[..., :width] + picked[..., width:]

def matmul(operand, matrix):
    return jnp.dot(
        operand, matrix, precision=lax.Precision.HIGH, preferred_element_type=jnp.float32
    )


def normalize(values, scale_row, shift_row):
    center = values - jnp.mean(values, axis=-1, keepdims=True)
    spread = jnp.mean(center * center, axis=-1, keepdims=True)
    return center * lax.rsqrt(spread + 1e-05) * scale_row + shift_row


def per_device(
    node_state,
    edge_state,
    sender,
    receiver,
    send_rows,
    step_owner,
    edge_weights,
    node_weights,
    step_bias,
    step_gain,
):
    node_rows = node_state
    edge_rows = edge_state
    rows_dev, features = node_rows.shape
    edges_dev = edge_rows.shape[0]
    directions = send_rows.shape[1]
    slots = send_rows.shape[2]
    windows = rows_dev // WIN
    per_window = edges_dev // windows
    me = lax.axis_index("dom") * lax.axis_size("sub") + lax.axis_index("sub")

    bank = jnp.concatenate([edge_weights[0], node_weights[0], step_bias[0], step_gain[0]], axis=0)
    me_dom = lax.axis_index("dom")
    n_sub = lax.axis_size("sub")
    row = lax.all_gather(bank, "sub")
    columns = [jnp.take(row, step_owner[number] % n_sub, axis=0) for number in range(STEPS)]
    banks = [spread(columns[0], step_owner[0] // n_sub)]
    late = [
        jnp.where(me_dom == step_owner[number] // n_sub, columns[number], jnp.zeros_like(columns[number]))
        for number in range(1, STEPS)
    ]
    late = lax.psum(jnp.stack(late), "dom")
    banks.extend(late[i] for i in range(STEPS - 1))

    offsets = (jnp.arange(windows, dtype=jnp.int32) * WIN)[:, None]
    relative = receiver.reshape(windows, per_window) - offsets
    incidence = (relative[:, :, None] == jnp.arange(WIN, dtype=jnp.int32)[None, None, :]).astype(
        jnp.float32
    )
    outgoing_rows = send_rows[0].reshape(-1)
    ghosts = directions * slots
    pick_local = (sender[:, None] == jnp.arange(rows_dev, dtype=jnp.int32)[None, :]).astype(
        jnp.bfloat16
    )
    pick_ghost = (
        sender[:, None] == rows_dev + jnp.arange(ghosts, dtype=jnp.int32)[None, :]
    ).astype(jnp.bfloat16)
    pick_target = incidence.astype(jnp.bfloat16)
    e_rows = 4 * features
    n_rows = 3 * features
    for number in range(STEPS):
        outgoing = jnp.take(node_rows, outgoing_rows, axis=0).reshape(directions, slots, features)
        dom_lower = from_behind(outgoing[0], "dom", 1)
        dom_upper = from_behind(outgoing[1], "dom", -1)
        sub_lower = from_behind(outgoing[2], "sub", 1)
        sub_upper = from_behind(outgoing[3], "sub", -1)
        arrived = jnp.concatenate([dom_lower, dom_upper, sub_lower, sub_upper], axis=0)

        weights = banks[number]
        w1 = weights[0:features]
        w2 = weights[features : 2 * features]
        w3 = weights[2 * features : 3 * features]
        w4 = weights[3 * features : e_rows]
        u1 = weights[e_rows : e_rows + features]
        u2 = weights[e_rows + features : e_rows + 2 * features]
        u3 = weights[e_rows + 2 * features : e_rows + n_rows]
        biases = weights[e_rows + n_rows : e_rows + n_rows + 6]
        gains = weights[e_rows + n_rows + 6 : e_rows + n_rows + 8]

        own_proj = matmul(node_rows, w2)
        ghost_proj = matmul(arrived, w2)
        source_proj = select_rows(pick_local, own_proj) + select_rows(pick_ghost, ghost_proj)
        target_proj = select_rows(
            pick_target, matmul(node_rows, w3).reshape(windows, WIN, features)
        ).reshape(edges_dev, features)
        hidden = matmul(edge_rows, w1) + source_proj
        hidden = hidden + target_proj + biases[0]
        hidden = jnp.maximum(hidden, 0.0)
        result_rows = matmul(hidden, w4) + biases[1]
        edge_rows = edge_rows + normalize(result_rows, gains[0], biases[2])

        incoming = jnp.einsum(
            "bew,bed->bwd",
            incidence,
            edge_rows.reshape(windows, per_window, features),
            precision=lax.Precision.HIGH,
            preferred_element_type=jnp.float32,
        ).reshape(rows_dev, features)
        hidden = matmul(node_rows, u1) + matmul(incoming, u2) + biases[3]
        hidden = jnp.maximum(hidden, 0.0)
        result_rows = matmul(hidden, u3) + biases[4]
        node_rows = node_rows + normalize(result_rows, gains[1], biases[5])
    return (node_rows, edge_rows)


def solution(mesh):
    in_specs = (
        P(AXES, None),
        P(AXES, None),
        P(AXES),
        P(AXES),
        P(AXES, None, None),
        P(),
        P(AXES, None, None),
        P(AXES, None, None),
        P(AXES, None, None),
        P(AXES, None, None),
    )
    out_specs = (P(AXES, None), P(AXES, None))
    return jax.shard_map(
        per_device, mesh=mesh, in_specs=in_specs, out_specs=out_specs, check_vma=False
    )
```

```python
import jax
import jax.numpy as jnp
from jax import lax
from jax.sharding import PartitionSpec as P

WIN = 128
STEPS = 4
AXES = ("dom", "sub")


def from_behind(block, axis, distance):
    devices = range(lax.axis_size(axis))
    route = [((i - distance) % len(devices), i) for i in devices]
    return lax.ppermute(block, axis, route)


def shift(block, axis, size, stride, step):
    count = lax.axis_size(axis)
    route = []
    for i in range(count):
        c = (i // stride) % size
        j = i + (((c + step) % size) - c) * stride
        route.append((i, j))
    return lax.ppermute(block, axis, route)


def spread(block, root):
    mine_all = lax.axis_index("dom")
    half = block.shape[0] // 2
    for size, stride in ((4, 1), (4, 4)):
        mine = (mine_all // stride) % size
        theirs = (root // stride) % size
        k = (mine - theirs + size) % size
        ahead = shift(block, "dom", size, stride, 1)
        behind = shift(block, "dom", size, stride, -1)
        block = jnp.where(k == 1, ahead, jnp.where(k == size - 1, behind, block))
        top = shift(block[:half], "dom", size, stride, 1)
        bottom = shift(block[half:], "dom", size, stride, -1)
        block = jnp.where(k == 2, jnp.concatenate([top, bottom], axis=0), block)
    return block


def select_rows(choice, table):
    first = lax.reduce_precision(table, exponent_bits=8, mantissa_bits=7)
    second = lax.reduce_precision(table - first, exponent_bits=8, mantissa_bits=7)
    parts = jnp.concatenate([first, second], axis=-1).astype(jnp.bfloat16)
    picked = jnp.matmul(choice, parts, preferred_element_type=jnp.float32)
    width = table.shape[-1]
    return picked[..., :width] + picked[..., width:]

def matmul(operand, matrix):
    return jnp.dot(
        operand, matrix, precision=lax.Precision.HIGH, preferred_element_type=jnp.float32
    )


def normalize(values, scale_row, shift_row):
    center = values - jnp.mean(values, axis=-1, keepdims=True)
    spread = jnp.mean(center * center, axis=-1, keepdims=True)
    return center * lax.rsqrt(spread + 1e-05) * scale_row + shift_row


def per_device(
    node_state,
    edge_state,
    sender,
    receiver,
    send_rows,
    step_owner,
    edge_weights,
    node_weights,
    step_bias,
    step_gain,
):
    node_rows = node_state
    edge_rows = edge_state
    rows_dev, features = node_rows.shape
    edges_dev = edge_rows.shape[0]
    directions = send_rows.shape[1]
    slots = send_rows.shape[2]
    windows = rows_dev // WIN
    per_window = edges_dev // windows
    me = lax.axis_index("dom") * lax.axis_size("sub") + lax.axis_index("sub")

    bank = jnp.concatenate([edge_weights[0], node_weights[0], step_bias[0], step_gain[0]], axis=0)
    me_dom = lax.axis_index("dom")
    n_sub = lax.axis_size("sub")
    row = lax.all_gather(bank, "sub")
    columns = [jnp.take(row, step_owner[number] % n_sub, axis=0) for number in range(STEPS)]
    banks = [spread(columns[0], step_owner[0] // n_sub)]
    late = [
        jnp.where(me_dom == step_owner[number] // n_sub, columns[number], jnp.zeros_like(columns[number]))
        for number in range(1, STEPS)
    ]
    late = lax.psum(jnp.stack(late), "dom")
    banks.extend(late[i] for i in range(STEPS - 1))

    offsets = (jnp.arange(windows, dtype=jnp.int32) * WIN)[:, None]
    relative = receiver.reshape(windows, per_window) - offsets
    incidence = (relative[:, :, None] == jnp.arange(WIN, dtype=jnp.int32)[None, None, :]).astype(
        jnp.float32
    )
    outgoing_rows = send_rows[0].reshape(-1)
    ghosts = directions * slots
    pick_local = (sender[:, None] == jnp.arange(rows_dev, dtype=jnp.int32)[None, :]).astype(
        jnp.bfloat16
    )
    pick_ghost = (
        sender[:, None] == rows_dev + jnp.arange(ghosts, dtype=jnp.int32)[None, :]
    ).astype(jnp.bfloat16)
    e_rows = 4 * features
    n_rows = 3 * features
    for number in range(STEPS):
        outgoing = jnp.take(node_rows, outgoing_rows, axis=0).reshape(directions, slots, features)
        dom_lower = from_behind(outgoing[0], "dom", 1)
        dom_upper = from_behind(outgoing[1], "dom", -1)
        sub_lower = from_behind(outgoing[2], "sub", 1)
        sub_upper = from_behind(outgoing[3], "sub", -1)
        arrived = jnp.concatenate([dom_lower, dom_upper, sub_lower, sub_upper], axis=0)

        weights = banks[number]
        w1 = weights[0:features]
        w2 = weights[features : 2 * features]
        w3 = weights[2 * features : 3 * features]
        w4 = weights[3 * features : e_rows]
        u1 = weights[e_rows : e_rows + features]
        u2 = weights[e_rows + features : e_rows + 2 * features]
        u3 = weights[e_rows + 2 * features : e_rows + n_rows]
        biases = weights[e_rows + n_rows : e_rows + n_rows + 6]
        gains = weights[e_rows + n_rows + 6 : e_rows + n_rows + 8]

        own_proj = matmul(node_rows, w2)
        ghost_proj = matmul(arrived, w2)
        source_proj = select_rows(pick_local, own_proj) + select_rows(pick_ghost, ghost_proj)
        target_proj = jnp.einsum(
            "bew,bwd->bed",
            incidence,
            matmul(node_rows, w3).reshape(windows, WIN, features),
            precision=lax.Precision.HIGH,
            preferred_element_type=jnp.float32,
        ).reshape(edges_dev, features)
        hidden = matmul(edge_rows, w1) + source_proj
        hidden = hidden + target_proj + biases[0]
        hidden = jnp.maximum(hidden, 0.0)
        result_rows = matmul(hidden, w4) + biases[1]
        edge_rows = edge_rows + normalize(result_rows, gains[0], biases[2])

        incoming = jnp.einsum(
            "bew,bed->bwd",
            incidence,
            edge_rows.reshape(windows, per_window, features),
            precision=lax.Precision.HIGH,
            preferred_element_type=jnp.float32,
        ).reshape(rows_dev, features)
        hidden = matmul(node_rows, u1) + matmul(incoming, u2) + biases[3]
        hidden = jnp.maximum(hidden, 0.0)
        result_rows = matmul(hidden, u3) + biases[4]
        node_rows = node_rows + normalize(result_rows, gains[1], biases[5])
    return (node_rows, edge_rows)


def solution(mesh):
    in_specs = (
        P(AXES, None),
        P(AXES, None),
        P(AXES),
        P(AXES),
        P(AXES, None, None),
        P(),
        P(AXES, None, None),
        P(AXES, None, None),
        P(AXES, None, None),
        P(AXES, None, None),
    )
    out_specs = (P(AXES, None), P(AXES, None))
    return jax.shard_map(
        per_device, mesh=mesh, in_specs=in_specs, out_specs=out_specs, check_vma=False
    )
```
